32 devices in a mesh: row: 4 (over z), col: 4 (over y, x), cuts: 2 (over core).
Axes of the slice: x: 2, y: 2, z: 4, core: 2. Of those that a mesh axis runs over, the one named last changes fastest.
Arguments:
- warm: float32 [40, 32768], P('cuts', ('row', 'col')), may hold values from -6 to 6
- tiles: float32 [5504, 128, 128], P(('row', 'col', 'cuts')), may hold values from -0.125 to 0.125
- tile_rows: int32 [5504], P(('row', 'col', 'cuts')), may hold values from -1 to 255, as said below
- tile_cols: int32 [5504], P(('row', 'col', 'cuts')), may hold values from 0 to 255, as said below
Outputs:
- basis: float32 [40, 32768], P('cuts', ('row', 'col'))
- residual: float32 [40, 32768], P('cuts', ('row', 'col'))
The draws below stay inside these ranges and needn't reach their ends.
Inputs may be any that keep to these rules, and one draw needn't show every extreme that they name: `tile_rows`: slots come in groups of 344; group r * (size of col) + c belongs to the grid position with row index r and column index c. A group's tiles lie in the block rows r * (size of col) * 16 up to (r + 1) * (size of col) * 16 - 1, and in block columns j with (j // 16) % (size of col) = c. No block appears twice. In each group the live slots come first and fill at least half of it; some group is full. Block rows hold uneven numbers of tiles. `tile_cols`: see tile_rows; an empty slot's column is that of some block the group may hold.
All inputs are finite; a program needn't handle non-finite values.
Results may differ from the reference program's by a relative error of at most 0.0003.
Values sent between devices are 32-bit elements; how exact they have to be, the bound alone decides.
No kernel may reach another device: no remote copies, remote signals or barrier semaphores. Data moves between devices by JAX's collectives and lax.ppermute only.
A program may use at most 64 MiB of HBM per device.

```python
import jax
import jax.numpy as jnp
from jax import lax

K = 40
BLOCK = 128
TILES_ROW = 16
SEG_BLOCKS = 16
SLOTS = 344
BLOCK_ROWS = 256
ITEMS = 32768
SLOTS_ALL = 5504
N_ROW = 4
N_COL = 4


def tile_pattern(key):
    devices = N_ROW * N_COL
    key = jax.random.fold_in(key, 4211)
    score_key, count_key, full_key = jax.random.split(key, 3)
    local_rows = N_COL * SEG_BLOCKS
    local_cols = N_ROW * SEG_BLOCKS
    candidates = local_rows * local_cols
    upper = max(2, (1 << 30) // candidates)
    scores = jax.random.randint(score_key, (devices, candidates), 0, upper) * candidates + jnp.arange(candidates, dtype=jnp.int32)[None, :]
    order = jnp.argsort(scores, axis=1, stable=True)[:, :SLOTS].astype(jnp.int32)
    counts = jax.random.randint(count_key, (devices,), SLOTS // 2, SLOTS + 1)
    busiest = jax.random.randint(full_key, (), 0, devices)
    counts = jnp.where(jnp.arange(devices) == busiest, SLOTS, counts)
    device = jnp.arange(devices, dtype=jnp.int32)[:, None]
    row_index = device // N_COL
    col_index = device % N_COL
    lrow = order // local_cols
    lcol = order % local_cols
    grow = row_index * N_COL * SEG_BLOCKS + lrow
    gcol = (lcol // SEG_BLOCKS * N_COL + col_index) * SEG_BLOCKS + lcol % SEG_BLOCKS
    live = jnp.arange(SLOTS, dtype=jnp.int32)[None, :] < counts[:, None]
    rows = jnp.where(live, grow, -1)
    return (rows.reshape(-1).astype(jnp.int32), gcol.reshape(-1).astype(jnp.int32))


def draw_tile_rows(key, part):
    return tile_pattern(key)[0]


def draw_tile_cols(key, part):
    return tile_pattern(key)[1]


def levels(own_key, extent, shards, smallest, high):
    def one(axis_at, blocks):
        steps = jax.random.uniform(jax.random.fold_in(jax.random.fold_in(own_key, 6), axis_at), (blocks,), jnp.float32, smallest / len(shards), high / len(shards))
        return jnp.repeat(jnp.exp(steps), extent[axis_at] // blocks).reshape((-1,) + (1,) * (len(extent) - axis_at - 1))

    gain = one(*shards[0])
    for cut in shards[1:]:
        gain = gain * one(*cut)
    return gain


def scatter_about(stream_key, shape, deviation, limit, cuts=(), held_as=jnp.bfloat16):
    gain = levels(stream_key, shape, cuts, -0.22, 0.18) if cuts else 1.0
    entries = jax.random.normal(stream_key, shape, jnp.float32) * deviation * gain
    return jnp.minimum(jnp.maximum(entries, -limit), limit).astype(held_as)


def setup_inputs(seed: int = 0) -> dict:
    keys = jax.random.split(jax.random.key(seed), 5)
    warm = scatter_about(keys[0], (K, ITEMS), 1.0, 6.0, ((0, 2), (1, 16)), jnp.float32)
    tiles = scatter_about(keys[1], (SLOTS_ALL, BLOCK, BLOCK), (TILES_ROW * BLOCK) ** -0.5, 0.125, ((0, 32),), jnp.float32)
    tile_rows = draw_tile_rows(jax.random.fold_in(keys[4], 71), 0)
    tile_cols = draw_tile_cols(jax.random.fold_in(keys[4], 71), 0)
    return {"warm": warm, "tiles": tiles, "tile_rows": tile_rows, "tile_cols": tile_cols}


def multiply(vectors, tiles, tile_rows, tile_cols):
    count_rows = vectors.shape[0]
    blocks = vectors.reshape(count_rows, BLOCK_ROWS, BLOCK)
    groups = N_ROW * N_COL

    def accumulate(total, pieces):
        tile_group, row_group, col_group = pieces
        picked = jnp.take(blocks, col_group.astype(jnp.int32), axis=1)
        prods = jnp.einsum('suv,ksv->ksu', tile_group, picked, precision=lax.Precision.HIGHEST)
        live = (row_group >= 0).astype(total.dtype)
        prods = prods * live[None, :, None]
        target = jnp.maximum(row_group, 0).astype(jnp.int32)
        summed = jax.ops.segment_sum(jnp.transpose(prods, (1, 0, 2)), target, num_segments=BLOCK_ROWS)
        return (total + summed, None)
    start = jnp.zeros((BLOCK_ROWS, count_rows, BLOCK), vectors.dtype)
    total, _ = lax.scan(accumulate, start, (tiles.reshape(groups, SLOTS, BLOCK, BLOCK), tile_rows.reshape(groups, SLOTS), tile_cols.reshape(groups, SLOTS)))
    return jnp.transpose(total, (1, 0, 2)).reshape(count_rows, ITEMS)

def reference(warm, tiles, tile_rows, tile_cols):
    image = multiply(warm, tiles, tile_rows, tile_cols)
    gram = jnp.dot(image.astype(jnp.float32), image.T.astype(jnp.float32), precision=lax.Precision.HIGHEST, preferred_element_type=jnp.float32) / ITEMS
    lower = jnp.linalg.cholesky(gram)
    basis = lax.linalg.triangular_solve(lower, image, left_side=True, lower=True)
    product = multiply(basis, tiles, tile_rows, tile_cols)
    projected = jnp.dot(basis.astype(jnp.float32), product.T.astype(jnp.float32), precision=lax.Precision.HIGHEST, preferred_element_type=jnp.float32) / ITEMS
    residual = product - jnp.dot(projected.T.astype(jnp.float32), basis.astype(jnp.float32), precision=lax.Precision.HIGHEST, preferred_element_type=jnp.float32)
    return (basis, residual)
```

```python
import functools

import jax
import jax.numpy as jnp
from jax import lax
from jax.experimental import pallas as pl
from jax.experimental.pallas import tpu as pltpu
from jax.sharding import PartitionSpec as P


HIGHEST = lax.Precision.HIGHEST
VM = pl.BlockSpec(memory_space=pltpu.VMEM)
SM = pl.BlockSpec(memory_space=pltpu.SMEM)
UNROLL = 12
PASSES = ((0,), (1, 2), (3,))


def f32(shape):
    return jax.ShapeDtypeStruct(shape, jnp.float32)


def dot(a, b, contract):
    return lax.dot_general(
        a, b, (contract, ((), ())), precision=HIGHEST, preferred_element_type=jnp.float32
    )


def call(kernel, outs, n_smem, *args, scratch=(), flops=10**7):
    nbytes = sum(x.size * 4 for x in args[n_smem:])
    return pl.pallas_call(
        kernel,
        out_shape=outs,
        in_specs=[SM] * n_smem + [VM] * (len(args) - n_smem),
        out_specs=jax.tree.map(lambda _: VM, outs),
        scratch_shapes=list(scratch),
        cost_estimate=pl.CostEstimate(flops=flops, bytes_accessed=nbytes, transcendentals=0),
        compiler_params=pltpu.CompilerParams(vmem_limit_bytes=24 << 20),
    )(*args)


def pass_kernel(n_x, first, last, order, rowp, colp, bounds, *refs):
    xs, refs = refs[:n_x], refs[n_x:]
    tiles, refs = refs[0], refs[1:]
    if not first:
        acc_in, refs = refs[0], refs[1:]
    if last:
        keep, send, panel, acc = refs
    else:
        acc, panel = refs
    begin, end = bounds[0], bounds[1]
    base = bounds[2]
    kk = xs[0].shape[1]
    nblk = xs[0].shape[0]
    total = acc.shape[0]

    def start(i, carry):
        acc[i] = jnp.zeros(acc.shape[1:], jnp.float32) if first else acc_in[i]
        return carry

    lax.fori_loop(0, total, start, 0, unroll=8)
    for q, x in enumerate(xs):
        for i in range(nblk):
            v = x[i]
            hi = v.astype(jnp.bfloat16).astype(jnp.float32)
            panel[q * nblk + i] = jnp.concatenate([hi, v - hi], axis=0).astype(jnp.bfloat16)

    def body(b, carry):
        outs = []
        for u in range(UNROLL):
            s = jnp.minimum(begin + b * UNROLL + u, end - 1)
            t = tiles[order[s]]
            hi = t.astype(jnp.bfloat16)
            lo = (t - hi.astype(jnp.float32)).astype(jnp.bfloat16)
            p = panel[colp[s] - base]
            d = lax.dot_general(
                jnp.concatenate([p, p], axis=1),
                jnp.concatenate([hi, lo], axis=1),
                (((1,), (1,)), ((), ())),
                preferred_element_type=jnp.float32,
            )
            outs.append(d[:kk] + d[kk:])
        for u in range(UNROLL):
            s = begin + b * UNROLL + u
            row = rowp[jnp.minimum(s, end - 1)]
            acc[row] = acc[row] + jnp.where(s < end, outs[u], 0.0)
        return carry

    lax.fori_loop(0, (end - begin + UNROLL - 1) // UNROLL, body, 0)
    if last:

        def finish(i, carry):
            keep[i] = acc[i]
            send[i] = acc[i + total // 2]
            return carry

        lax.fori_loop(0, total // 2, finish, 0, unroll=8)


def apply_pass(index, xs, tiles, acc, out_blocks, last):
    order, rowp, colp, bounds = index
    nblk, kk, block = xs[0].shape
    first = acc is None
    half = f32((out_blocks // 2, kk, block))
    whole = f32((out_blocks, kk, block))
    scratch = [pltpu.VMEM((len(xs) * nblk, 2 * kk, block), jnp.bfloat16)]
    if last:
        scratch.append(pltpu.VMEM((out_blocks, kk, block), jnp.float32))
    return call(
        functools.partial(pass_kernel, len(xs), first, last),
        (half, half) if last else whole,
        4,
        order, rowp, colp, bounds, *xs, tiles, *(() if first else (acc,)),
        scratch=scratch,
        flops=10**9,
    )


def wide(ref):
    return jnp.concatenate([ref[i] for i in range(ref.shape[0])], axis=1)


def pad_lanes(x):
    return jnp.concatenate([x, jnp.zeros((x.shape[0], 128 - x.shape[1]), x.dtype)], axis=1)


def enter_kernel(core, warm, recv, x):
    own = core[0] == 0
    blocks, _, block = x.shape
    for i in range(blocks):
        low = warm[:, i * block:(i + 1) * block]
        high = warm[:, (blocks + i) * block:(blocks + i + 1) * block]
        mine = jnp.where(own, low, high)
        got = recv[:, i * block:(i + 1) * block]
        x[i] = jnp.concatenate([jnp.where(own, mine, got), jnp.where(own, got, mine)], axis=0)


def gram_kernel(*refs):
    xs, out = refs[:-1], refs[-1]
    total = None
    for x in xs:
        v = wide(x)
        g = dot(v, v, ((1,), (1,)))
        total = g if total is None else total + g
    out[...] = pad_lanes(total)


def inverse_kernel(items, gram, out):
    k = gram.shape[0]
    row = lax.broadcasted_iota(jnp.int32, (k, 128), 0)
    lane = lax.broadcasted_iota(jnp.int32, (k, 128), 1)
    m = jnp.where(lane < k, gram[...] / items, jnp.where(lane == row + 64, 1.0, 0.0))
    for j in range(k):
        scale = 1.0 / jnp.sqrt(m[j:j + 1, j:j + 1])
        pivot = m[j:j + 1, :] * scale
        column = m[:, j:j + 1] * scale
        m = jnp.where(row == j, pivot, jnp.where(row > j, m - column * pivot, m))
    out[...] = pad_lanes(m[:, 64:64 + k])


def split_rows(own, v, keep, send):
    h = v.shape[0] // 2
    top, low = v[:h], v[h:]
    keep[...] = jnp.where(own, top, low)
    send[...] = jnp.where(own, low, top)


def basis_kernel(core, inverse, image, basis, keep, send):
    k = image.shape[1]
    v = dot(inverse[:, :k], wide(image), ((1,), (0,)))
    basis[...] = v
    split_rows(core[0] == 0, v, keep, send)


def product_kernel(inverse, raw, basis, product, partial):
    k = raw.shape[1]
    v = dot(inverse[:, :k], wide(raw), ((1,), (0,)))
    product[...] = v
    partial[...] = pad_lanes(dot(basis[...], v, ((1,), (1,))))


def residual_kernel(items, core, product, basis, projected, keep, send):
    k = basis.shape[0]
    p = projected[:, :k] / items
    v = product[...] - dot(p, basis[...], ((0,), (0,)))
    split_rows(core[0] == 0, v, keep, send)


def swap(x, axis, bit):
    n = lax.axis_size(axis)
    return lax.ppermute(x, axis, [(i, i ^ bit) for i in range(n)])


def swap_cross(x, first, second):
    n = lax.axis_size("col")
    pairs = []
    for c in range(n):
        pairs.append((c * 2, (c ^ first) * 2))
        pairs.append((c * 2 + 1, (c ^ second) * 2 + 1))
    return lax.ppermute(x, ("col", "cuts"), pairs)


def gather(x):
    near = swap(x, "row", 1)
    far = swap(x, "row", 2)
    last = swap(far, "row", 1)
    own = {0: x, 1: near, 2: far, 3: last}
    both = {}
    for rel, value in own.items():
        both[rel] = (value, swap(value, "cuts", 1))
    return both


def operator(index, tiles, shards_of, out_blocks):
    acc = None
    for q, rels in enumerate(PASSES):
        xs = [x for rel in rels for x in shards_of[rel]]
        acc = apply_pass(
            (*index[:3], index[3][q]), xs, tiles, acc, out_blocks, q == len(PASSES) - 1
        )
    return acc


def reduce(keep, send):
    got = swap(send, "cuts", 1)
    n = keep.shape[0]
    away = keep[n // 2:] + got[n // 2:]
    first = swap_cross(away, 1, 2)
    stay = n // 4
    pass_on = keep[stay:n // 2] + got[stay:n // 2] + first[stay:]
    second = swap_cross(pass_on, 2, 1)
    return keep[:stay] + got[:stay] + first[:stay] + second


def schedule(tile_rows, tile_cols, seg_blocks):
    ncol = lax.axis_size("col")
    r, c, a = (lax.axis_index(n) for n in ("row", "col", "cuts"))
    half = seg_blocks // 2
    slots = tile_rows.shape[0]
    col_half = tile_cols % seg_blocks // half
    rel = (tile_cols // seg_blocks // ncol) ^ r
    colp = (rel * 2 + (col_half ^ a)) * half + tile_cols % half
    local = tile_rows - r * ncol * seg_blocks
    live = tile_rows >= 0
    d = (local // seg_blocks) ^ c
    owner = local % seg_blocks // half
    place = jnp.where(owner == 0, d // 2 + d % 2 * 2, d)
    rowp = ((owner ^ a) * ncol + place) * half + local % half
    rowp = jnp.where(live, rowp, 0)
    key = jnp.where(live, (rel + 1) // 2, len(PASSES))
    ids = lax.iota(jnp.int32, slots)
    rank = key * slots + ids
    place_of = jnp.sum((rank[None, :] < rank[:, None]).astype(jnp.int32), axis=1)
    onehot = place_of[None, :] == ids[:, None]

    def pick(v):
        return jnp.sum(jnp.where(onehot, v[None, :], 0), axis=1)

    edges = [jnp.sum((key < q).astype(jnp.int32)) for q in range(len(PASSES) + 1)]
    bounds = [
        jnp.stack([edges[q], edges[q + 1], jnp.int32(rels[0] * 2 * half)])
        for q, rels in enumerate(PASSES)
    ]
    return pick(ids), pick(rowp), pick(colp), bounds


def fast_shards(warm, tiles, tile_rows, tile_cols):
    ncol, nrow = lax.axis_size("col"), lax.axis_size("row")
    a = lax.axis_index("cuts")
    block = tiles.shape[1]
    kloc, width = warm.shape
    k = 2 * kloc
    seg_blocks = width // block
    half = seg_blocks // 2
    out_blocks = ncol * seg_blocks
    items = width * nrow * ncol
    core = jnp.reshape(a, (1,)).astype(jnp.int32)

    away = jnp.where(a == 0, warm[:, width // 2:], warm[:, :width // 2])
    got = swap(away, "cuts", 1)
    x = call(enter_kernel, f32((half, k, block)), 1, core, warm, got)
    index = schedule(tile_rows, tile_cols, seg_blocks)
    keep, send = operator(index, tiles, gather(x), out_blocks)
    image = reduce(keep, send)
    panel = gather(image)
    keep, send = operator(index, tiles, panel, out_blocks)

    halves = [h for rel in range(nrow) for h in panel[rel]]
    gram = call(gram_kernel, f32((k, 128)), 0, *halves)
    gram = gram + swap(gram, "col", 1)
    gram = gram + swap(gram, "col", 2)
    inverse = call(functools.partial(inverse_kernel, items), f32((k, 128)), 0, gram)
    part = f32((kloc, width // 2))
    full = f32((k, width // 2))
    basis, basis_keep, basis_send = call(
        basis_kernel, (full, part, part), 1, core, inverse, image
    )

    raw = reduce(keep, send)
    product, partial = call(product_kernel, (full, f32((k, 128))), 0, inverse, raw, basis)
    for axis, bit in (("cuts", 1), ("col", 1), ("col", 2), ("row", 1), ("row", 2)):
        partial = partial + swap(partial, axis, bit)
    res_keep, res_send = call(
        functools.partial(residual_kernel, items), (part, part), 1, core, product, basis, partial
    )

    def joined(mine, away):
        other = swap(away, "cuts", 1)
        return jnp.where(
            a == 0,
            jnp.concatenate([mine, other], axis=1),
            jnp.concatenate([other, mine], axis=1),
        )

    return joined(basis_keep, basis_send), joined(res_keep, res_send)


def block_product(panel, tiles, rows, positions, base, out_blocks):
    count_rows = panel.shape[0]
    block = tiles.shape[1]
    blocks = panel.reshape(count_rows, -1, block)
    picked = jnp.take(blocks, positions, axis=1)
    prods = jnp.einsum("suv,ksv->ksu", tiles, picked, precision=HIGHEST)
    local = rows - base
    onehot = (local[:, None] == jnp.arange(out_blocks, dtype=jnp.int32)[None, :]).astype(
        jnp.float32
    )
    summed = jnp.einsum("ksu,sb->kbu", prods, onehot, precision=HIGHEST)
    return summed.reshape(count_rows, out_blocks * block)


def operator_apply(vectors, tiles, rows, positions, base, out_blocks):
    panel = lax.all_gather(vectors, "row", axis=1, tiled=True)
    panel = lax.all_gather(panel, "cuts", axis=0, tiled=True)
    partial_value = block_product(panel, tiles, rows, positions, base, out_blocks)
    partial_value = lax.psum_scatter(partial_value, "cuts", scatter_dimension=0, tiled=True)
    return lax.psum_scatter(partial_value, "col", scatter_dimension=1, tiled=True)


def any_shards(warm, tiles, tile_rows, tile_cols):
    ncol = lax.axis_size("col")
    nrow = lax.axis_size("row")
    block = tiles.shape[1]
    seg_blocks = warm.shape[1] // block
    out_blocks = ncol * seg_blocks
    items = warm.shape[1] * nrow * ncol
    base = lax.axis_index("row") * out_blocks
    segment = tile_cols // seg_blocks
    positions = segment // ncol * seg_blocks + tile_cols % seg_blocks
    image = operator_apply(warm, tiles, tile_rows, positions, base, out_blocks)
    whole = lax.all_gather(image, "cuts", axis=0, tiled=True)
    gram = lax.psum(dot(whole, whole, ((1,), (1,))), ("row", "col")) / items
    lower = jnp.linalg.cholesky(gram)
    kloc = warm.shape[0]
    start = lax.axis_index("cuts") * kloc
    inverse = lax.linalg.triangular_solve(
        lower, jnp.eye(whole.shape[0], dtype=jnp.float32), left_side=True, lower=True
    )
    mine_rows = lax.dynamic_slice_in_dim(inverse, start, kloc, 0)
    basis = dot(mine_rows, whole, ((1,), (0,)))
    basis_all = lax.all_gather(basis, "cuts", axis=0, tiled=True)
    product = operator_apply(basis, tiles, tile_rows, positions, base, out_blocks)
    projected = lax.psum(dot(basis_all, product, ((1,), (1,))), ("row", "col")) / items
    residual = product - dot(projected, basis_all, ((0,), (0,)))
    return (basis, residual)


def solution(mesh):
    sizes = tuple(mesh.shape[n] for n in ("row", "col", "cuts"))
    return jax.shard_map(
        fast_shards if sizes == (4, 4, 2) else any_shards,
        mesh=mesh,
        in_specs=(
            P("cuts", ("row", "col")),
            P(("row", "col", "cuts"), None, None),
            P(("row", "col", "cuts")),
            P(("row", "col", "cuts")),
        ),
        out_specs=(P("cuts", ("row", "col")), P("cuts", ("row", "col"))),
        check_vma=False,
    )
```

```python
import functools

import jax
import jax.numpy as jnp
from jax import lax
from jax.experimental import pallas as pl
from jax.experimental.pallas import tpu as pltpu
from jax.sharding import PartitionSpec as P


HIGHEST = lax.Precision.HIGHEST
VM = pl.BlockSpec(memory_space=pltpu.VMEM)
SM = pl.BlockSpec(memory_space=pltpu.SMEM)
UNROLL = 12
PASSES = ((0,), (1, 2), (3,))


def f32(shape):
    return jax.ShapeDtypeStruct(shape, jnp.float32)


def dot(a, b, contract):
    return lax.dot_general(
        a, b, (contract, ((), ())), precision=HIGHEST, preferred_element_type=jnp.float32
    )


def call(kernel, outs, n_smem, *args, scratch=(), flops=10**7):
    nbytes = sum(x.size * 4 for x in args[n_smem:])
    return pl.pallas_call(
        kernel,
        out_shape=outs,
        in_specs=[SM] * n_smem + [VM] * (len(args) - n_smem),
        out_specs=jax.tree.map(lambda _: VM, outs),
        scratch_shapes=list(scratch),
        cost_estimate=pl.CostEstimate(flops=flops, bytes_accessed=nbytes, transcendentals=0),
        compiler_params=pltpu.CompilerParams(vmem_limit_bytes=24 << 20),
    )(*args)


def stage_kernel(chunk, depth, tiles, out, buf, sems):
    steps = tiles.shape[0] // chunk

    def copy(i):
        slot = lax.rem(i, depth)
        return pltpu.make_async_copy(
            tiles.at[pl.ds(i * chunk, chunk)], buf.at[slot], sems.at[slot]
        )

    for i in range(min(depth - 1, steps)):
        copy(i).start()

    def body(i, carry):
        @pl.when(i + depth - 1 < steps)
        def _():
            copy(i + depth - 1).start()

        copy(i).wait()
        slot = lax.rem(i, depth)
        for q in range(chunk):
            t = buf[slot, q]
            hi = t.astype(jnp.bfloat16)
            lo = (t - hi.astype(jnp.float32)).astype(jnp.bfloat16)
            out[i * chunk + q] = jnp.concatenate([hi, lo], axis=1)
        return carry

    lax.fori_loop(0, steps, body, 0)


def stage(tiles):
    slots, block, _ = tiles.shape
    chunk = max(q for q in range(1, 9) if slots % q == 0)
    depth = 4
    return pl.pallas_call(
        functools.partial(stage_kernel, chunk, depth),
        out_shape=jax.ShapeDtypeStruct((slots, block, 2 * block), jnp.bfloat16),
        in_specs=[pl.BlockSpec(memory_space=pltpu.HBM)],
        out_specs=VM,
        scratch_shapes=[
            pltpu.VMEM((depth, chunk, block, block), jnp.float32),
            pltpu.SemaphoreType.DMA((depth,)),
        ],
        cost_estimate=pl.CostEstimate(
            flops=0, bytes_accessed=tiles.size * 4, transcendentals=0
        ),
        compiler_params=pltpu.CompilerParams(vmem_limit_bytes=24 << 20),
    )(pltpu.with_memory_space_constraint(tiles, pltpu.HBM))


def pass_kernel(n_x, first, by_items, q, base, core, order, rowp, colp, edges, *refs):
    xs, refs = refs[:n_x], refs[n_x:]
    tiles, refs = refs[0], refs[1:]
    if not first:
        acc_in, refs = refs[0], refs[1:]
    acc, panel = refs
    begin, end = edges[q], edges[q + 1]
    kk = acc.shape[1]
    own = core[0] == 0

    def start(i, carry):
        acc[i] = jnp.zeros(acc.shape[1:], jnp.float32) if first else acc_in[i]
        return carry

    lax.fori_loop(0, acc.shape[0], start, 0, unroll=8)

    def put(i, v):
        hi = v.astype(jnp.bfloat16).astype(jnp.float32)
        panel[i] = jnp.concatenate([hi, v - hi], axis=0).astype(jnp.bfloat16)

    for g in range(n_x // 2):
        mine, other = xs[2 * g], xs[2 * g + 1]
        if by_items:
            n = mine.shape[0]
            for i in range(n):
                put(2 * g * n + i, jnp.where(own, mine[i], other[i]))
                put((2 * g + 1) * n + i, jnp.where(own, other[i], mine[i]))
        else:
            h = kk // 2
            n = mine.shape[0] // h
            for i in range(n):
                m, o = mine[i * h:(i + 1) * h], other[i * h:(i + 1) * h]
                put(g * n + i, jnp.concatenate([jnp.where(own, m, o), jnp.where(own, o, m)], 0))

    def body(b, carry):
        outs = []
        for u in range(UNROLL):
            s = jnp.minimum(begin + b * UNROLL + u, end - 1)
            p = panel[colp[s] - base]
            d = lax.dot_general(
                jnp.concatenate([p, p], axis=1),
                tiles[order[s]],
                (((1,), (1,)), ((), ())),
                preferred_element_type=jnp.float32,
            )
            outs.append(d[:kk] + d[kk:])
        for u in range(UNROLL):
            s = begin + b * UNROLL + u
            row = rowp[jnp.minimum(s, end - 1)]
            acc[row] = acc[row] + jnp.where(s < end, outs[u], 0.0)
        return carry

    lax.fori_loop(0, (end - begin + UNROLL - 1) // UNROLL, body, 0)


def operator(core, index, tiles, shards_of, k, out_blocks, seg_blocks, by_items):
    block = tiles.shape[1]
    acc = None
    for q, rels in enumerate(PASSES):
        xs = [x for rel in rels for x in shards_of[rel]]
        first = acc is None
        acc = call(
            functools.partial(
                pass_kernel, len(xs), first, by_items, q, rels[0] * seg_blocks
            ),
            f32((out_blocks, k, block)),
            5,
            core, *index, *xs, tiles, *(() if first else (acc,)),
            scratch=[pltpu.VMEM((len(rels) * seg_blocks, 2 * k, block), jnp.bfloat16)],
            flops=10**9,
        )
    return acc


def wide(ref):
    return jnp.concatenate([ref[i] for i in range(ref.shape[0])], axis=1)


def pad_lanes(x):
    return jnp.concatenate([x, jnp.zeros((x.shape[0], 128 - x.shape[1]), x.dtype)], axis=1)


def enter_kernel(warm, x):
    h = warm.shape[0]
    for i in range(x.shape[0] // h):
        x[i * h:(i + 1) * h] = warm[:, i * 128:(i + 1) * 128]


def outer_kernel(n, *refs):
    left = jnp.concatenate([wide(r) for r in refs[:n]], axis=1)
    right = jnp.concatenate([wide(r) for r in refs[n:-1]], axis=1) if len(refs) > n + 1 else left
    refs[-1][...] = pad_lanes(dot(left, right, ((1,), (1,))))


def outer(left, right):
    k = left[0].shape[1]
    return call(functools.partial(outer_kernel, len(left)), f32((k, 128)), 0, *left, *right)


def inverse_kernel(items, gram, out):
    k = gram.shape[0]
    row = lax.broadcasted_iota(jnp.int32, (k, 128), 0)
    lane = lax.broadcasted_iota(jnp.int32, (k, 128), 1)
    m = jnp.where(lane < k, gram[...] / items, jnp.where(lane == row + 64, 1.0, 0.0))
    for j in range(k):
        scale = 1.0 / jnp.sqrt(m[j:j + 1, j:j + 1])
        pivot = m[j:j + 1, :] * scale
        column = m[:, j:j + 1] * scale
        m = jnp.where(row == j, pivot, jnp.where(row > j, m - column * pivot, m))
    out[...] = pad_lanes(m[:, 64:64 + k])


def in_order(own, mine, other):
    a, b = wide(mine), wide(other)
    return jnp.concatenate([jnp.where(own, a, b), jnp.where(own, b, a)], axis=1)


def own_rows(own, v):
    h = v.shape[0] // 2
    return jnp.where(own, v[:h], v[h:])


def basis_kernel(core, inverse, image, other, basis, out):
    k = inverse.shape[0]
    own = core[0] == 0
    v = dot(inverse[:, :k], in_order(own, image, other), ((1,), (0,)))
    basis[...] = v
    out[...] = own_rows(own, v)


def residual_kernel(items, core, inverse, cross, raw, other, basis, out):
    k = basis.shape[0]
    own = core[0] == 0
    inv = inverse[:, :k]
    projected = dot(dot(inv, cross[:, :k] / items, ((1,), (0,))), inv, ((1,), (1,)))
    product = dot(own_rows(own, inv), in_order(own, raw, other), ((1,), (0,)))
    out[...] = product - dot(own_rows(own, projected.T), basis[...], ((1,), (0,)))


def swap(x, axis, bit):
    n = lax.axis_size(axis)
    return lax.ppermute(x, axis, [(i, i ^ bit) for i in range(n)])


def swap_cross(x, first, second):
    n = lax.axis_size("col")
    pairs = []
    for c in range(n):
        pairs.append((c * 2, (c ^ first) * 2))
        pairs.append((c * 2 + 1, (c ^ second) * 2 + 1))
    return lax.ppermute(x, ("col", "cuts"), pairs)


def gather(x):
    far = swap(x, "row", 2)
    near = swap(x, "row", 1)
    last = swap(far, "row", 1)
    return {rel: (v, swap(v, "cuts", 1)) for rel, v in ((0, x), (1, near), (2, far), (3, last))}


def reduce_cuts(acc):
    n = acc.shape[0]
    got = swap(acc[n // 2:], "cuts", 1)
    return acc[:n // 4] + got[:n // 4], acc[n // 4:n // 2] + got[n // 4:]


def reduce_col(stay, away):
    first = swap_cross(away, 1, 2)
    n = stay.shape[0] // 2
    second = swap_cross(stay[n:] + first[n:], 2, 1)
    return stay[:n] + first[:n] + second


def total(x, order):
    for axis, bit in order:
        x = x + swap(x, axis, bit)
    return x


def schedule(tile_rows, tile_cols, seg_blocks):
    ncol = lax.axis_size("col")
    r, c, a = (lax.axis_index(n) for n in ("row", "col", "cuts"))
    half = seg_blocks // 2
    slots = tile_rows.shape[0]
    rel = (tile_cols // seg_blocks // ncol) ^ r
    colp = rel * seg_blocks + tile_cols % seg_blocks
    local = tile_rows - r * ncol * seg_blocks
    live = tile_rows >= 0
    d = (local // seg_blocks) ^ c
    owner = local % seg_blocks // half
    place = jnp.where(owner == 0, d // 2 + d % 2 * 2, d)
    rowp = ((owner ^ a) * ncol + place) * half + local % half
    key = jnp.where(live, (rel + 1) // 2, len(PASSES))
    ids = lax.iota(jnp.int32, slots)
    rank = key * slots + ids
    place_of = jnp.sum((rank[None, :] < rank[:, None]).astype(jnp.int32), axis=1)
    onehot = place_of[None, :] == ids[:, None]
    packed = jnp.where(live, rowp * 256 + colp, 0)
    order = jnp.sum(jnp.where(onehot, ids[None, :], 0), axis=1)
    packed = jnp.sum(jnp.where(onehot, packed[None, :], 0), axis=1)
    marks = lax.iota(jnp.int32, len(PASSES) + 1)
    edges = jnp.sum((key[None, :] < marks[:, None]).astype(jnp.int32), axis=1)
    return order, packed // 256, packed % 256, edges


def fast_shards(warm, tiles, tile_rows, tile_cols):
    ncol, nrow = lax.axis_size("col"), lax.axis_size("row")
    block = tiles.shape[1]
    kloc, width = warm.shape
    k = 2 * kloc
    seg_blocks = width // block
    out_blocks = ncol * seg_blocks
    items = width * nrow * ncol
    core = jnp.reshape(lax.axis_index("cuts"), (1,)).astype(jnp.int32)

    x = call(enter_kernel, f32((seg_blocks * kloc, block)), 0, warm)
    staged = stage(tiles)
    index = schedule(tile_rows, tile_cols, seg_blocks)
    sizes = (k, out_blocks, seg_blocks)
    acc = operator(core, index, staged, gather(x), *sizes, False)
    stay, away = reduce_cuts(acc)
    image = reduce_col(stay, away)

    panel = gather(image)
    gram = outer([image], [])
    gram = total(gram, (("cuts", 1), ("col", 1), ("col", 2), ("row", 1), ("row", 2)))
    beside = swap_cross(image, 2, 1)
    across = swap_cross(jnp.concatenate([image, beside]), 1, 2)
    acc = operator(core, index, staged, panel, *sizes, True)
    stay, away = reduce_cuts(acc)
    cross = outer([image, beside, across], [stay, away])
    cross = total(cross, (("row", 1), ("row", 2), ("cuts", 1), ("col", 1), ("col", 2)))
    inverse = call(functools.partial(inverse_kernel, items), f32((k, 128)), 0, gram)
    basis_all, basis = call(
        basis_kernel, (f32((k, width)), f32((kloc, width))), 1,
        core, inverse, *panel[0],
    )
    raw = reduce_col(stay, away)
    other = swap(raw, "cuts", 1)
    residual = call(
        functools.partial(residual_kernel, items), f32((kloc, width)), 1,
        core, inverse, cross, raw, other, basis_all,
    )
    return basis, residual


def block_product(panel, tiles, rows, positions, base, out_blocks):
    count_rows = panel.shape[0]
    block = tiles.shape[1]
    blocks = panel.reshape(count_rows, -1, block)
    picked = jnp.take(blocks, positions, axis=1)
    prods = jnp.einsum("suv,ksv->ksu", tiles, picked, precision=HIGHEST)
    local = rows - base
    onehot = (local[:, None] == jnp.arange(out_blocks, dtype=jnp.int32)[None, :]).astype(
        jnp.float32
    )
    summed = jnp.einsum("ksu,sb->kbu", prods, onehot, precision=HIGHEST)
    return summed.reshape(count_rows, out_blocks * block)


def operator_apply(vectors, tiles, rows, positions, base, out_blocks):
    panel = lax.all_gather(vectors, "row", axis=1, tiled=True)
    panel = lax.all_gather(panel, "cuts", axis=0, tiled=True)
    partial_value = block_product(panel, tiles, rows, positions, base, out_blocks)
    partial_value = lax.psum_scatter(partial_value, "cuts", scatter_dimension=0, tiled=True)
    return lax.psum_scatter(partial_value, "col", scatter_dimension=1, tiled=True)


def any_shards(warm, tiles, tile_rows, tile_cols):
    ncol = lax.axis_size("col")
    nrow = lax.axis_size("row")
    block = tiles.shape[1]
    seg_blocks = warm.shape[1] // block
    out_blocks = ncol * seg_blocks
    items = warm.shape[1] * nrow * ncol
    base = lax.axis_index("row") * out_blocks
    segment = tile_cols // seg_blocks
    positions = segment // ncol * seg_blocks + tile_cols % seg_blocks
    image = operator_apply(warm, tiles, tile_rows, positions, base, out_blocks)
    whole = lax.all_gather(image, "cuts", axis=0, tiled=True)
    gram = lax.psum(dot(whole, whole, ((1,), (1,))), ("row", "col")) / items
    lower = jnp.linalg.cholesky(gram)
    kloc = warm.shape[0]
    start = lax.axis_index("cuts") * kloc
    inverse = lax.linalg.triangular_solve(
        lower, jnp.eye(whole.shape[0], dtype=jnp.float32), left_side=True, lower=True
    )
    mine_rows = lax.dynamic_slice_in_dim(inverse, start, kloc, 0)
    basis = dot(mine_rows, whole, ((1,), (0,)))
    basis_all = lax.all_gather(basis, "cuts", axis=0, tiled=True)
    product = operator_apply(basis, tiles, tile_rows, positions, base, out_blocks)
    projected = lax.psum(dot(basis_all, product, ((1,), (1,))), ("row", "col")) / items
    residual = product - dot(projected, basis_all, ((0,), (0,)))
    return (basis, residual)


def solution(mesh):
    sizes = tuple(mesh.shape[n] for n in ("row", "col", "cuts"))
    fast = sizes == (4, 4, 2)
    return jax.shard_map(
        fast_shards if fast else any_shards,
        mesh=mesh,
        in_specs=(
            P("cuts", ("row", "col")),
            P(("row", "col", "cuts"), None, None),
            P(("row", "col", "cuts")),
            P(("row", "col", "cuts")),
        ),
        out_specs=(P("cuts", ("row", "col")), P("cuts", ("row", "col"))),
        check_vma=False,
    )
```

```python
import functools

import jax
import jax.numpy as jnp
from jax import lax
from jax.experimental import pallas as pl
from jax.experimental.pallas import tpu as pltpu
from jax.sharding import PartitionSpec as P


HIGHEST = lax.Precision.HIGHEST
VM = pl.BlockSpec(memory_space=pltpu.VMEM)
SM = pl.BlockSpec(memory_space=pltpu.SMEM)
UNROLL = 12
PASSES = ((0,), (1, 2), (3,))


def f32(shape):
    return jax.ShapeDtypeStruct(shape, jnp.float32)


def dot(a, b, contract):
    return lax.dot_general(
        a, b, (contract, ((), ())), precision=HIGHEST, preferred_element_type=jnp.float32
    )


def call(kernel, outs, n_smem, *args, scratch=(), flops=10**7):
    nbytes = sum(x.size * 4 for x in args[n_smem:])
    return pl.pallas_call(
        kernel,
        out_shape=outs,
        in_specs=[SM] * n_smem + [VM] * (len(args) - n_smem),
        out_specs=jax.tree.map(lambda _: VM, outs),
        scratch_shapes=list(scratch),
        cost_estimate=pl.CostEstimate(flops=flops, bytes_accessed=nbytes, transcendentals=0),
        compiler_params=pltpu.CompilerParams(vmem_limit_bytes=24 << 20),
    )(*args)


def stage_kernel(parts, tiles, out, sems):
    n = tiles.shape[0]
    edges = [n * q // parts for q in range(parts + 1)]
    copies = [
        pltpu.make_async_copy(tiles.at[pl.ds(a, b - a)], out.at[pl.ds(a, b - a)], sems.at[q])
        for q, (a, b) in enumerate(zip(edges, edges[1:]))
    ]
    for copy in copies:
        copy.start()
    for copy in copies:
        copy.wait()


def stage(tiles):
    parts = 8
    return pl.pallas_call(
        functools.partial(stage_kernel, parts),
        out_shape=f32(tiles.shape),
        in_specs=[pl.BlockSpec(memory_space=pltpu.HBM)],
        out_specs=VM,
        scratch_shapes=[pltpu.SemaphoreType.DMA((parts,))],
        cost_estimate=pl.CostEstimate(
            flops=0, bytes_accessed=tiles.size * 4, transcendentals=0
        ),
        compiler_params=pltpu.CompilerParams(vmem_limit_bytes=24 << 20),
    )(pltpu.with_memory_space_constraint(tiles, pltpu.HBM))


def pass_kernel(n_x, first, by_items, q, base, core, order, rowp, colp, edges, *refs):
    xs, refs = refs[:n_x], refs[n_x:]
    tiles, refs = refs[0], refs[1:]
    if not first:
        acc_in, refs = refs[0], refs[1:]
    acc, panel = refs
    begin, end = edges[q], edges[q + 1]
    kk = acc.shape[1]
    own = core[0] == 0

    def start(i, carry):
        acc[i] = jnp.zeros(acc.shape[1:], jnp.float32) if first else acc_in[i]
        return carry

    lax.fori_loop(0, acc.shape[0], start, 0, unroll=8)

    def put(i, v):
        hi = v.astype(jnp.bfloat16).astype(jnp.float32)
        panel[i] = jnp.concatenate([hi, v - hi], axis=0).astype(jnp.bfloat16)

    for g in range(n_x // 2):
        mine, other = xs[2 * g], xs[2 * g + 1]
        if by_items:
            n = mine.shape[0]
            for i in range(n):
                put(2 * g * n + i, jnp.where(own, mine[i], other[i]))
                put((2 * g + 1) * n + i, jnp.where(own, other[i], mine[i]))
        else:
            h = kk // 2
            n = mine.shape[0] // h
            for i in range(n):
                m, o = mine[i * h:(i + 1) * h], other[i * h:(i + 1) * h]
                put(g * n + i, jnp.concatenate([jnp.where(own, m, o), jnp.where(own, o, m)], 0))

    def body(b, carry):
        outs = []
        for u in range(UNROLL):
            s = jnp.minimum(begin + b * UNROLL + u, end - 1)
            p = panel[colp[s] - base]
            t = tiles[order[s]]
            hi = t.astype(jnp.bfloat16)
            lo = (t - hi.astype(jnp.float32)).astype(jnp.bfloat16)
            d = lax.dot_general(
                jnp.concatenate([p, p], axis=1),
                jnp.concatenate([hi, lo], axis=1),
                (((1,), (1,)), ((), ())),
                preferred_element_type=jnp.float32,
            )
            outs.append(d[:kk] + d[kk:])
        for u in range(UNROLL):
            s = begin + b * UNROLL + u
            row = rowp[jnp.minimum(s, end - 1)]
            acc[row] = acc[row] + jnp.where(s < end, outs[u], 0.0)
        return carry

    lax.fori_loop(0, (end - begin + UNROLL - 1) // UNROLL, body, 0)


def operator(core, index, tiles, shards_of, k, out_blocks, seg_blocks, by_items):
    block = tiles.shape[1]
    acc = None
    for q, rels in enumerate(PASSES):
        xs = [x for rel in rels for x in shards_of[rel]]
        first = acc is None
        acc = call(
            functools.partial(
                pass_kernel, len(xs), first, by_items, q, rels[0] * seg_blocks
            ),
            f32((out_blocks, k, block)),
            5,
            core, *index, *xs, tiles, *(() if first else (acc,)),
            scratch=[pltpu.VMEM((len(rels) * seg_blocks, 2 * k, block), jnp.bfloat16)],
            flops=10**9,
        )
    return acc


def wide(ref):
    return jnp.concatenate([ref[i] for i in range(ref.shape[0])], axis=1)


def pad_lanes(x):
    return jnp.concatenate([x, jnp.zeros((x.shape[0], 128 - x.shape[1]), x.dtype)], axis=1)


def enter_kernel(warm, x):
    h = warm.shape[0]
    for i in range(x.shape[0] // h):
        x[i * h:(i + 1) * h] = warm[:, i * 128:(i + 1) * 128]


def outer_kernel(n, *refs):
    left = jnp.concatenate([wide(r) for r in refs[:n]], axis=1)
    right = jnp.concatenate([wide(r) for r in refs[n:-1]], axis=1) if len(refs) > n + 1 else left
    refs[-1][...] = pad_lanes(dot(left, right, ((1,), (1,))))


def outer(left, right):
    k = left[0].shape[1]
    return call(functools.partial(outer_kernel, len(left)), f32((k, 128)), 0, *left, *right)


def inverse_kernel(items, gram, out):
    k = gram.shape[0]
    row = lax.broadcasted_iota(jnp.int32, (k, 128), 0)
    lane = lax.broadcasted_iota(jnp.int32, (k, 128), 1)
    m = jnp.where(lane < k, gram[...] / items, jnp.where(lane == row + 64, 1.0, 0.0))
    for j in range(k):
        scale = 1.0 / jnp.sqrt(m[j:j + 1, j:j + 1])
        pivot = m[j:j + 1, :] * scale
        column = m[:, j:j + 1] * scale
        m = jnp.where(row == j, pivot, jnp.where(row > j, m - column * pivot, m))
    out[...] = pad_lanes(m[:, 64:64 + k])


def in_order(own, mine, other):
    a, b = wide(mine), wide(other)
    return jnp.concatenate([jnp.where(own, a, b), jnp.where(own, b, a)], axis=1)


def own_rows(own, v):
    h = v.shape[0] // 2
    return jnp.where(own, v[:h], v[h:])


def basis_kernel(core, inverse, image, other, basis, out):
    k = inverse.shape[0]
    own = core[0] == 0
    v = dot(inverse[:, :k], in_order(own, image, other), ((1,), (0,)))
    basis[...] = v
    out[...] = own_rows(own, v)


def residual_kernel(items, core, inverse, cross, raw, other, basis, out):
    k = basis.shape[0]
    own = core[0] == 0
    inv = inverse[:, :k]
    projected = dot(dot(inv, cross[:, :k] / items, ((1,), (0,))), inv, ((1,), (1,)))
    product = dot(own_rows(own, inv), in_order(own, raw, other), ((1,), (0,)))
    out[...] = product - dot(own_rows(own, projected.T), basis[...], ((1,), (0,)))


def swap(x, axis, bit):
    n = lax.axis_size(axis)
    return lax.ppermute(x, axis, [(i, i ^ bit) for i in range(n)])


def swap_cross(x, first, second):
    n = lax.axis_size("col")
    pairs = []
    for c in range(n):
        pairs.append((c * 2, (c ^ first) * 2))
        pairs.append((c * 2 + 1, (c ^ second) * 2 + 1))
    return lax.ppermute(x, ("col", "cuts"), pairs)


def gather(x):
    far = swap(x, "row", 2)
    near = swap(x, "row", 1)
    last = swap(far, "row", 1)
    return {rel: (v, swap(v, "cuts", 1)) for rel, v in ((0, x), (1, near), (2, far), (3, last))}


def reduce_cuts(acc):
    n = acc.shape[0]
    got = swap(acc[n // 2:], "cuts", 1)
    return acc[:n // 4] + got[:n // 4], acc[n // 4:n // 2] + got[n // 4:]


def reduce_col(stay, away):
    first = swap_cross(away, 1, 2)
    n = stay.shape[0] // 2
    second = swap_cross(stay[n:] + first[n:], 2, 1)
    return stay[:n] + first[:n] + second


def total(x, order):
    for axis, bit in order:
        x = x + swap(x, axis, bit)
    return x


def schedule(tile_rows, tile_cols, seg_blocks):
    ncol = lax.axis_size("col")
    r, c, a = (lax.axis_index(n) for n in ("row", "col", "cuts"))
    half = seg_blocks // 2
    slots = tile_rows.shape[0]
    rel = (tile_cols // seg_blocks // ncol) ^ r
    colp = rel * seg_blocks + tile_cols % seg_blocks
    local = tile_rows - r * ncol * seg_blocks
    live = tile_rows >= 0
    d = (local // seg_blocks) ^ c
    owner = local % seg_blocks // half
    place = jnp.where(owner == 0, d // 2 + d % 2 * 2, d)
    rowp = ((owner ^ a) * ncol + place) * half + local % half
    key = jnp.where(live, (rel + 1) // 2, len(PASSES))
    ids = lax.iota(jnp.int32, slots)
    rank = key * slots + ids
    place_of = jnp.sum((rank[None, :] < rank[:, None]).astype(jnp.int32), axis=1)
    onehot = place_of[None, :] == ids[:, None]
    packed = jnp.where(live, rowp * 256 + colp, 0)
    order = jnp.sum(jnp.where(onehot, ids[None, :], 0), axis=1)
    packed = jnp.sum(jnp.where(onehot, packed[None, :], 0), axis=1)
    marks = lax.iota(jnp.int32, len(PASSES) + 1)
    edges = jnp.sum((key[None, :] < marks[:, None]).astype(jnp.int32), axis=1)
    return order, packed // 256, packed % 256, edges


def fast_shards(warm, tiles, tile_rows, tile_cols):
    ncol, nrow = lax.axis_size("col"), lax.axis_size("row")
    block = tiles.shape[1]
    kloc, width = warm.shape
    k = 2 * kloc
    seg_blocks = width // block
    out_blocks = ncol * seg_blocks
    items = width * nrow * ncol
    core = jnp.reshape(lax.axis_index("cuts"), (1,)).astype(jnp.int32)

    x = call(enter_kernel, f32((seg_blocks * kloc, block)), 0, warm)
    staged = stage(tiles)
    index = schedule(tile_rows, tile_cols, seg_blocks)
    sizes = (k, out_blocks, seg_blocks)
    acc = operator(core, index, staged, gather(x), *sizes, False)
    stay, away = reduce_cuts(acc)
    image = reduce_col(stay, away)

    panel = gather(image)
    gram = outer([image], [])
    gram = total(gram, (("cuts", 1), ("col", 1), ("col", 2), ("row", 1), ("row", 2)))
    beside = swap_cross(image, 2, 1)
    across = swap_cross(jnp.concatenate([image, beside]), 1, 2)
    acc = operator(core, index, staged, panel, *sizes, True)
    stay, away = reduce_cuts(acc)
    cross = outer([image, beside, across], [stay, away])
    cross = total(cross, (("row", 1), ("row", 2), ("cuts", 1), ("col", 1), ("col", 2)))
    inverse = call(functools.partial(inverse_kernel, items), f32((k, 128)), 0, gram)
    basis_all, basis = call(
        basis_kernel, (f32((k, width)), f32((kloc, width))), 1,
        core, inverse, *panel[0],
    )
    raw = reduce_col(stay, away)
    other = swap(raw, "cuts", 1)
    residual = call(
        functools.partial(residual_kernel, items), f32((kloc, width)), 1,
        core, inverse, cross, raw, other, basis_all,
    )
    return basis, residual


def block_product(panel, tiles, rows, positions, base, out_blocks):
    count_rows = panel.shape[0]
    block = tiles.shape[1]
    blocks = panel.reshape(count_rows, -1, block)
    picked = jnp.take(blocks, positions, axis=1)
    prods = jnp.einsum("suv,ksv->ksu", tiles, picked, precision=HIGHEST)
    local = rows - base
    onehot = (local[:, None] == jnp.arange(out_blocks, dtype=jnp.int32)[None, :]).astype(
        jnp.float32
    )
    summed = jnp.einsum("ksu,sb->kbu", prods, onehot, precision=HIGHEST)
    return summed.reshape(count_rows, out_blocks * block)


def operator_apply(vectors, tiles, rows, positions, base, out_blocks):
    panel = lax.all_gather(vectors, "row", axis=1, tiled=True)
    panel = lax.all_gather(panel, "cuts", axis=0, tiled=True)
    partial_value = block_product(panel, tiles, rows, positions, base, out_blocks)
    partial_value = lax.psum_scatter(partial_value, "cuts", scatter_dimension=0, tiled=True)
    return lax.psum_scatter(partial_value, "col", scatter_dimension=1, tiled=True)


def any_shards(warm, tiles, tile_rows, tile_cols):
    ncol = lax.axis_size("col")
    nrow = lax.axis_size("row")
    block = tiles.shape[1]
    seg_blocks = warm.shape[1] // block
    out_blocks = ncol * seg_blocks
    items = warm.shape[1] * nrow * ncol
    base = lax.axis_index("row") * out_blocks
    segment = tile_cols // seg_blocks
    positions = segment // ncol * seg_blocks + tile_cols % seg_blocks
    image = operator_apply(warm, tiles, tile_rows, positions, base, out_blocks)
    whole = lax.all_gather(image, "cuts", axis=0, tiled=True)
    gram = lax.psum(dot(whole, whole, ((1,), (1,))), ("row", "col")) / items
    lower = jnp.linalg.cholesky(gram)
    kloc = warm.shape[0]
    start = lax.axis_index("cuts") * kloc
    inverse = lax.linalg.triangular_solve(
        lower, jnp.eye(whole.shape[0], dtype=jnp.float32), left_side=True, lower=True
    )
    mine_rows = lax.dynamic_slice_in_dim(inverse, start, kloc, 0)
    basis = dot(mine_rows, whole, ((1,), (0,)))
    basis_all = lax.all_gather(basis, "cuts", axis=0, tiled=True)
    product = operator_apply(basis, tiles, tile_rows, positions, base, out_blocks)
    projected = lax.psum(dot(basis_all, product, ((1,), (1,))), ("row", "col")) / items
    residual = product - dot(projected, basis_all, ((0,), (0,)))
    return (basis, residual)


def solution(mesh):
    sizes = tuple(mesh.shape[n] for n in ("row", "col", "cuts"))
    fast = sizes == (4, 4, 2)
    return jax.shard_map(
        fast_shards if fast else any_shards,
        mesh=mesh,
        in_specs=(
            P("cuts", ("row", "col")),
            P(("row", "col", "cuts"), None, None),
            P(("row", "col", "cuts")),
            P(("row", "col", "cuts")),
        ),
        out_specs=(P("cuts", ("row", "col")), P("cuts", ("row", "col"))),
        check_vma=False,
    )
```

```python
import functools

import jax
import jax.numpy as jnp
from jax import lax
from jax.experimental import pallas as pl
from jax.experimental.pallas import tpu as pltpu
from jax.sharding import PartitionSpec as P


HIGHEST = lax.Precision.HIGHEST
VM = pl.BlockSpec(memory_space=pltpu.VMEM)
SM = pl.BlockSpec(memory_space=pltpu.SMEM)
UNROLL = 12
PASSES = ((0,), (1, 2), (3,))


def f32(shape):
    return jax.ShapeDtypeStruct(shape, jnp.float32)


def dot(a, b, contract):
    return lax.dot_general(
        a, b, (contract, ((), ())), precision=HIGHEST, preferred_element_type=jnp.float32
    )


def call(kernel, outs, n_smem, *args, scratch=(), flops=10**7):
    nbytes = sum(x.size * 4 for x in args[n_smem:])
    return pl.pallas_call(
        kernel,
        out_shape=outs,
        in_specs=[SM] * n_smem + [VM] * (len(args) - n_smem),
        out_specs=jax.tree.map(lambda _: VM, outs),
        scratch_shapes=list(scratch),
        cost_estimate=pl.CostEstimate(flops=flops, bytes_accessed=nbytes, transcendentals=0),
        compiler_params=pltpu.CompilerParams(vmem_limit_bytes=24 << 20),
    )(*args)


def stage_kernel(parts, tiles, out, sems):
    n = tiles.shape[0]
    edges = [n * q // parts for q in range(parts + 1)]
    copies = [
        pltpu.make_async_copy(tiles.at[pl.ds(a, b - a)], out.at[pl.ds(a, b - a)], sems.at[q])
        for q, (a, b) in enumerate(zip(edges, edges[1:]))
    ]
    for copy in copies:
        copy.start()
    for copy in copies:
        copy.wait()


def stage(tiles):
    parts = 8
    return pl.pallas_call(
        functools.partial(stage_kernel, parts),
        out_shape=f32(tiles.shape),
        in_specs=[pl.BlockSpec(memory_space=pltpu.HBM)],
        out_specs=VM,
        scratch_shapes=[pltpu.SemaphoreType.DMA((parts,))],
        cost_estimate=pl.CostEstimate(
            flops=0, bytes_accessed=tiles.size * 4, transcendentals=0
        ),
        compiler_params=pltpu.CompilerParams(vmem_limit_bytes=24 << 20),
    )(pltpu.with_memory_space_constraint(tiles, pltpu.HBM))


def pass_kernel(n_x, first, by_items, q, base, core, order, rowp, colp, edges, *refs):
    xs, refs = refs[:n_x], refs[n_x:]
    tiles, refs = refs[0], refs[1:]
    if not first:
        acc_in, refs = refs[0], refs[1:]
    acc, panel = refs
    begin, end = edges[q], edges[q + 1]
    kk = acc.shape[1]
    own = core[0] == 0

    def start(i, carry):
        acc[i] = jnp.zeros(acc.shape[1:], jnp.float32) if first else acc_in[i]
        return carry

    lax.fori_loop(0, acc.shape[0], start, 0, unroll=8)

    def put(i, v):
        hi = v.astype(jnp.bfloat16).astype(jnp.float32)
        panel[i] = jnp.concatenate([hi, v - hi], axis=0).astype(jnp.bfloat16)

    for g in range(n_x // 2):
        mine, other = xs[2 * g], xs[2 * g + 1]
        if by_items:
            n = mine.shape[0]
            for i in range(n):
                put(2 * g * n + i, jnp.where(own, mine[i], other[i]))
                put((2 * g + 1) * n + i, jnp.where(own, other[i], mine[i]))
        else:
            h = kk // 2
            n = mine.shape[0] // h
            for i in range(n):
                m, o = mine[i * h:(i + 1) * h], other[i * h:(i + 1) * h]
                put(g * n + i, jnp.concatenate([jnp.where(own, m, o), jnp.where(own, o, m)], 0))

    def body(b, carry):
        outs = []
        for u in range(UNROLL):
            s = jnp.minimum(begin + b * UNROLL + u, end - 1)
            p = panel[colp[s] - base]
            t = tiles[order[s]]
            hi = t.astype(jnp.bfloat16)
            lo = (t - hi.astype(jnp.float32)).astype(jnp.bfloat16)
            d = lax.dot_general(
                jnp.concatenate([p, p], axis=1),
                jnp.concatenate([hi, lo], axis=1),
                (((1,), (1,)), ((), ())),
                preferred_element_type=jnp.float32,
            )
            outs.append(d[:kk] + d[kk:])
        for u in range(UNROLL):
            s = begin + b * UNROLL + u
            row = rowp[jnp.minimum(s, end - 1)]
            acc[row] = acc[row] + jnp.where(s < end, outs[u], 0.0)
        return carry

    lax.fori_loop(0, (end - begin + UNROLL - 1) // UNROLL, body, 0)


def operator(core, index, tiles, shards_of, k, out_blocks, seg_blocks, by_items):
    block = tiles.shape[1]
    acc = None
    for q, rels in enumerate(PASSES):
        xs = [x for rel in rels for x in shards_of[rel]]
        first = acc is None
        acc = call(
            functools.partial(
                pass_kernel, len(xs), first, by_items, q, rels[0] * seg_blocks
            ),
            f32((out_blocks, k, block)),
            5,
            core, *index, *xs, tiles, *(() if first else (acc,)),
            scratch=[pltpu.VMEM((len(rels) * seg_blocks, 2 * k, block), jnp.bfloat16)],
            flops=10**9,
        )
    return acc


def wide(ref):
    return jnp.concatenate([ref[i] for i in range(ref.shape[0])], axis=1)


def pad_lanes(x):
    return jnp.concatenate([x, jnp.zeros((x.shape[0], 128 - x.shape[1]), x.dtype)], axis=1)


def enter_kernel(warm, x):
    h = warm.shape[0]
    for i in range(x.shape[0] // h):
        x[i * h:(i + 1) * h] = warm[:, i * 128:(i + 1) * 128]


def outer_kernel(n, *refs):
    left = jnp.concatenate([wide(r) for r in refs[:n]], axis=1)
    right = jnp.concatenate([wide(r) for r in refs[n:-1]], axis=1) if len(refs) > n + 1 else left
    refs[-1][...] = pad_lanes(dot(left, right, ((1,), (1,))))


def outer(left, right):
    k = left[0].shape[1]
    return call(functools.partial(outer_kernel, len(left)), f32((k, 128)), 0, *left, *right)


def inverse_kernel(items, gram, out):
    k = gram.shape[0]
    row = lax.broadcasted_iota(jnp.int32, (k, 128), 0)
    lane = lax.broadcasted_iota(jnp.int32, (k, 128), 1)
    m = jnp.where(lane < k, gram[...] / items, jnp.where(lane == row + 64, 1.0, 0.0))
    for j in range(k):
        scale = 1.0 / jnp.sqrt(m[j:j + 1, j:j + 1])
        pivot = m[j:j + 1, :] * scale
        column = m[:, j:j + 1] * scale
        m = jnp.where(row == j, pivot, jnp.where(row > j, m - column * pivot, m))
    out[...] = pad_lanes(m[:, 64:64 + k])


def in_order(own, mine, other):
    a, b = wide(mine), wide(other)
    return jnp.concatenate([jnp.where(own, a, b), jnp.where(own, b, a)], axis=1)


def own_rows(own, v):
    h = v.shape[0] // 2
    return jnp.where(own, v[:h], v[h:])


def basis_kernel(core, inverse, image, other, basis, out):
    k = inverse.shape[0]
    own = core[0] == 0
    v = dot(inverse[:, :k], in_order(own, image, other), ((1,), (0,)))
    basis[...] = v
    out[...] = own_rows(own, v)


def residual_kernel(items, core, inverse, cross, raw, other, basis, out):
    k = basis.shape[0]
    own = core[0] == 0
    inv = inverse[:, :k]
    projected = dot(dot(inv, cross[:, :k] / items, ((1,), (0,))), inv, ((1,), (1,)))
    product = dot(own_rows(own, inv), in_order(own, raw, other), ((1,), (0,)))
    out[...] = product - dot(own_rows(own, projected.T), basis[...], ((1,), (0,)))


def swap(x, axis, bit):
    n = lax.axis_size(axis)
    return lax.ppermute(x, axis, [(i, i ^ bit) for i in range(n)])


def swap_cross(x, first, second):
    n = lax.axis_size("col")
    pairs = []
    for c in range(n):
        pairs.append((c * 2, (c ^ first) * 2))
        pairs.append((c * 2 + 1, (c ^ second) * 2 + 1))
    return lax.ppermute(x, ("col", "cuts"), pairs)


def gather(x):
    far = swap(x, "row", 2)
    near = swap(x, "row", 1)
    last = swap(far, "row", 1)
    return {rel: (v, swap(v, "cuts", 1)) for rel, v in ((0, x), (1, near), (2, far), (3, last))}


def reduce_cuts(acc, ncol):
    n = acc.shape[0] // 2
    got = swap(acc[n:], "cuts", 1)
    step = n // ncol
    return [
        lax.optimization_barrier(acc[q * step:(q + 1) * step] + got[q * step:(q + 1) * step])
        for q in range(ncol)
    ]


def reduce_col(parts):
    far = swap_cross(parts[3], 3, 3)
    one = swap_cross(parts[1], 2, 1)
    two = swap_cross(parts[2], 1, 2)
    return parts[0] + one + two + far


def total(x, order):
    for axis, bit in order:
        x = x + swap(x, axis, bit)
    return x


def schedule(tile_rows, tile_cols, seg_blocks):
    ncol = lax.axis_size("col")
    r, c, a = (lax.axis_index(n) for n in ("row", "col", "cuts"))
    half = seg_blocks // 2
    slots = tile_rows.shape[0]
    rel = (tile_cols // seg_blocks // ncol) ^ r
    colp = rel * seg_blocks + tile_cols % seg_blocks
    local = tile_rows - r * ncol * seg_blocks
    live = tile_rows >= 0
    d = (local // seg_blocks) ^ c
    owner = local % seg_blocks // half
    place = jnp.where(owner == 0, d // 2 + d % 2 * 2, d)
    rowp = ((owner ^ a) * ncol + place) * half + local % half
    key = jnp.where(live, (rel + 1) // 2, len(PASSES))
    ids = lax.iota(jnp.int32, slots)
    rank = key * slots + ids
    place_of = jnp.sum((rank[None, :] < rank[:, None]).astype(jnp.int32), axis=1)
    onehot = place_of[None, :] == ids[:, None]
    packed = jnp.where(live, rowp * 256 + colp, 0)
    order = jnp.sum(jnp.where(onehot, ids[None, :], 0), axis=1)
    packed = jnp.sum(jnp.where(onehot, packed[None, :], 0), axis=1)
    marks = lax.iota(jnp.int32, len(PASSES) + 1)
    edges = jnp.sum((key[None, :] < marks[:, None]).astype(jnp.int32), axis=1)
    return order, packed // 256, packed % 256, edges


def fast_shards(warm, tiles, tile_rows, tile_cols):
    ncol, nrow = lax.axis_size("col"), lax.axis_size("row")
    block = tiles.shape[1]
    kloc, width = warm.shape
    k = 2 * kloc
    seg_blocks = width // block
    out_blocks = ncol * seg_blocks
    items = width * nrow * ncol
    core = jnp.reshape(lax.axis_index("cuts"), (1,)).astype(jnp.int32)

    x = call(enter_kernel, f32((seg_blocks * kloc, block)), 0, warm)
    staged = stage(tiles)
    index = schedule(tile_rows, tile_cols, seg_blocks)
    sizes = (k, out_blocks, seg_blocks)
    acc = operator(core, index, staged, gather(x), *sizes, False)
    image = reduce_col(reduce_cuts(acc, ncol))

    panel = gather(image)
    beside = swap_cross(image, 2, 1)
    across = swap_cross(jnp.concatenate([image, beside]), 1, 2)
    acc = operator(core, index, staged, panel, *sizes, True)
    parts = reduce_cuts(acc, ncol)
    gram = 0.0
    for rels in PASSES:
        gram += outer([x for rel in rels for x in panel[rel]], [])
    gram = total(gram, (("col", 1), ("col", 2)))
    cross = outer([image, beside, across], parts)
    cross = total(cross, (("row", 1), ("row", 2), ("cuts", 1), ("col", 1), ("col", 2)))
    inverse = call(functools.partial(inverse_kernel, items), f32((k, 128)), 0, gram)
    basis_all, basis = call(
        basis_kernel, (f32((k, width)), f32((kloc, width))), 1,
        core, inverse, *panel[0],
    )
    raw = reduce_col(parts)
    other = swap(raw, "cuts", 1)
    residual = call(
        functools.partial(residual_kernel, items), f32((kloc, width)), 1,
        core, inverse, cross, raw, other, basis_all,
    )
    return basis, residual


def block_product(panel, tiles, rows, positions, base, out_blocks):
    count_rows = panel.shape[0]
    block = tiles.shape[1]
    blocks = panel.reshape(count_rows, -1, block)
    picked = jnp.take(blocks, positions, axis=1)
    prods = jnp.einsum("suv,ksv->ksu", tiles, picked, precision=HIGHEST)
    local = rows - base
    onehot = (local[:, None] == jnp.arange(out_blocks, dtype=jnp.int32)[None, :]).astype(
        jnp.float32
    )
    summed = jnp.einsum("ksu,sb->kbu", prods, onehot, precision=HIGHEST)
    return summed.reshape(count_rows, out_blocks * block)


def operator_apply(vectors, tiles, rows, positions, base, out_blocks):
    panel = lax.all_gather(vectors, "row", axis=1, tiled=True)
    panel = lax.all_gather(panel, "cuts", axis=0, tiled=True)
    partial_value = block_product(panel, tiles, rows, positions, base, out_blocks)
    partial_value = lax.psum_scatter(partial_value, "cuts", scatter_dimension=0, tiled=True)
    return lax.psum_scatter(partial_value, "col", scatter_dimension=1, tiled=True)


def any_shards(warm, tiles, tile_rows, tile_cols):
    ncol = lax.axis_size("col")
    nrow = lax.axis_size("row")
    block = tiles.shape[1]
    seg_blocks = warm.shape[1] // block
    out_blocks = ncol * seg_blocks
    items = warm.shape[1] * nrow * ncol
    base = lax.axis_index("row") * out_blocks
    segment = tile_cols // seg_blocks
    positions = segment // ncol * seg_blocks + tile_cols % seg_blocks
    image = operator_apply(warm, tiles, tile_rows, positions, base, out_blocks)
    whole = lax.all_gather(image, "cuts", axis=0, tiled=True)
    gram = lax.psum(dot(whole, whole, ((1,), (1,))), ("row", "col")) / items
    lower = jnp.linalg.cholesky(gram)
    kloc = warm.shape[0]
    start = lax.axis_index("cuts") * kloc
    inverse = lax.linalg.triangular_solve(
        lower, jnp.eye(whole.shape[0], dtype=jnp.float32), left_side=True, lower=True
    )
    mine_rows = lax.dynamic_slice_in_dim(inverse, start, kloc, 0)
    basis = dot(mine_rows, whole, ((1,), (0,)))
    basis_all = lax.all_gather(basis, "cuts", axis=0, tiled=True)
    product = operator_apply(basis, tiles, tile_rows, positions, base, out_blocks)
    projected = lax.psum(dot(basis_all, product, ((1,), (1,))), ("row", "col")) / items
    residual = product - dot(projected, basis_all, ((0,), (0,)))
    return (basis, residual)


def solution(mesh):
    sizes = tuple(mesh.shape[n] for n in ("row", "col", "cuts"))
    fast = sizes == (4, 4, 2)
    return jax.shard_map(
        fast_shards if fast else any_shards,
        mesh=mesh,
        in_specs=(
            P("cuts", ("row", "col")),
            P(("row", "col", "cuts"), None, None),
            P(("row", "col", "cuts")),
            P(("row", "col", "cuts")),
        ),
        out_specs=(P("cuts", ("row", "col")), P("cuts", ("row", "col"))),
        check_vma=False,
    )
```

```python
import functools

import jax
import jax.numpy as jnp
from jax import lax
from jax.experimental import pallas as pl
from jax.experimental.pallas import tpu as pltpu
from jax.sharding import PartitionSpec as P


HIGHEST = lax.Precision.HIGHEST
VM = pl.BlockSpec(memory_space=pltpu.VMEM)
SM = pl.BlockSpec(memory_space=pltpu.SMEM)
UNROLL = 12
PASSES = ((0,), (1, 2), (3,))


def f32(shape):
    return jax.ShapeDtypeStruct(shape, jnp.float32)


def dot(a, b, contract):
    return lax.dot_general(
        a, b, (contract, ((), ())), precision=HIGHEST, preferred_element_type=jnp.float32
    )


def call(kernel, outs, n_smem, *args, scratch=(), flops=10**7):
    nbytes = sum(x.size * 4 for x in args[n_smem:])
    return pl.pallas_call(
        kernel,
        out_shape=outs,
        in_specs=[SM] * n_smem + [VM] * (len(args) - n_smem),
        out_specs=jax.tree.map(lambda _: VM, outs),
        scratch_shapes=list(scratch),
        cost_estimate=pl.CostEstimate(flops=flops, bytes_accessed=nbytes, transcendentals=0),
        compiler_params=pltpu.CompilerParams(vmem_limit_bytes=24 << 20),
    )(*args)


def stage_kernel(parts, tiles, out, sems):
    n = tiles.shape[0]
    edges = [n * q // parts for q in range(parts + 1)]
    copies = [
        pltpu.make_async_copy(tiles.at[pl.ds(a, b - a)], out.at[pl.ds(a, b - a)], sems.at[q])
        for q, (a, b) in enumerate(zip(edges, edges[1:]))
    ]
    for copy in copies:
        copy.start()
    for copy in copies:
        copy.wait()


def stage(tiles):
    parts = 8
    return pl.pallas_call(
        functools.partial(stage_kernel, parts),
        out_shape=f32(tiles.shape),
        in_specs=[pl.BlockSpec(memory_space=pltpu.HBM)],
        out_specs=VM,
        scratch_shapes=[pltpu.SemaphoreType.DMA((parts,))],
        cost_estimate=pl.CostEstimate(
            flops=0, bytes_accessed=tiles.size * 4, transcendentals=0
        ),
        compiler_params=pltpu.CompilerParams(vmem_limit_bytes=24 << 20),
    )(pltpu.with_memory_space_constraint(tiles, pltpu.HBM))


def pass_kernel(n_x, first, by_items, q, base, core, order, rowp, colp, edges, *refs):
    xs, refs = refs[:n_x], refs[n_x:]
    tiles, refs = refs[0], refs[1:]
    if not first:
        acc_in, refs = refs[0], refs[1:]
    acc, panel = refs
    begin, end = edges[q], edges[q + 1]
    kk = acc.shape[1]
    own = core[0] == 0

    def start(i, carry):
        acc[i] = jnp.zeros(acc.shape[1:], jnp.float32) if first else acc_in[i]
        return carry

    lax.fori_loop(0, acc.shape[0], start, 0, unroll=8)

    def put(i, v):
        hi = v.astype(jnp.bfloat16).astype(jnp.float32)
        panel[i] = jnp.concatenate([hi, v - hi], axis=0).astype(jnp.bfloat16)

    for g in range(n_x // 2):
        mine, other = xs[2 * g], xs[2 * g + 1]
        if by_items:
            n = mine.shape[0]
            for i in range(n):
                put(2 * g * n + i, jnp.where(own, mine[i], other[i]))
                put((2 * g + 1) * n + i, jnp.where(own, other[i], mine[i]))
        else:
            h = kk // 2
            n = mine.shape[0] // h
            for i in range(n):
                m, o = mine[i * h:(i + 1) * h], other[i * h:(i + 1) * h]
                put(g * n + i, jnp.concatenate([jnp.where(own, m, o), jnp.where(own, o, m)], 0))

    def body(b, carry):
        outs = []
        for u in range(UNROLL):
            s = jnp.minimum(begin + b * UNROLL + u, end - 1)
            p = panel[colp[s] - base]
            t = tiles[order[s]]
            hi = t.astype(jnp.bfloat16)
            lo = (t - hi.astype(jnp.float32)).astype(jnp.bfloat16)
            d = lax.dot_general(
                jnp.concatenate([p, p], axis=1),
                jnp.concatenate([hi, lo], axis=1),
                (((1,), (1,)), ((), ())),
                preferred_element_type=jnp.float32,
            )
            outs.append(d[:kk] + d[kk:])
        for u in range(UNROLL):
            s = begin + b * UNROLL + u
            row = rowp[jnp.minimum(s, end - 1)]
            acc[row] = acc[row] + jnp.where(s < end, outs[u], 0.0)
        return carry

    lax.fori_loop(0, (end - begin + UNROLL - 1) // UNROLL, body, 0)


def operator(core, index, tiles, shards_of, k, out_blocks, seg_blocks, by_items):
    block = tiles.shape[1]
    acc = None
    for q, rels in enumerate(PASSES):
        xs = [x for rel in rels for x in shards_of[rel]]
        first = acc is None
        acc = call(
            functools.partial(
                pass_kernel, len(xs), first, by_items, q, rels[0] * seg_blocks
            ),
            f32((out_blocks, k, block)),
            5,
            core, *index, *xs, tiles, *(() if first else (acc,)),
            scratch=[pltpu.VMEM((len(rels) * seg_blocks, 2 * k, block), jnp.bfloat16)],
            flops=10**9,
        )
    return acc


def wide(ref):
    return jnp.concatenate([ref[i] for i in range(ref.shape[0])], axis=1)


def pad_lanes(x):
    return jnp.concatenate([x, jnp.zeros((x.shape[0], 128 - x.shape[1]), x.dtype)], axis=1)


def enter_kernel(warm, x):
    h = warm.shape[0]
    for i in range(x.shape[0] // h):
        x[i * h:(i + 1) * h] = warm[:, i * 128:(i + 1) * 128]


def outer_kernel(n, *refs):
    left = jnp.concatenate([wide(r) for r in refs[:n]], axis=1)
    right = jnp.concatenate([wide(r) for r in refs[n:-1]], axis=1) if len(refs) > n + 1 else left
    refs[-1][...] = pad_lanes(dot(left, right, ((1,), (1,))))


def outer(left, right):
    k = left[0].shape[1]
    return call(functools.partial(outer_kernel, len(left)), f32((k, 128)), 0, *left, *right)


def inverse_kernel(items, gram, out):
    k = gram.shape[0]
    row = lax.broadcasted_iota(jnp.int32, (k, 128), 0)
    lane = lax.broadcasted_iota(jnp.int32, (k, 128), 1)
    m = jnp.where(lane < k, gram[...] / items, jnp.where(lane == row + 64, 1.0, 0.0))
    for j in range(k):
        scale = 1.0 / jnp.sqrt(m[j:j + 1, j:j + 1])
        pivot = m[j:j + 1, :] * scale
        column = m[:, j:j + 1] * scale
        m = jnp.where(row == j, pivot, jnp.where(row > j, m - column * pivot, m))
    out[...] = pad_lanes(m[:, 64:64 + k])


def in_order(own, mine, other):
    a, b = wide(mine), wide(other)
    return jnp.concatenate([jnp.where(own, a, b), jnp.where(own, b, a)], axis=1)


def own_rows(own, v):
    h = v.shape[0] // 2
    return jnp.where(own, v[:h], v[h:])


def basis_kernel(core, inverse, image, other, basis, out):
    k = inverse.shape[0]
    own = core[0] == 0
    v = dot(inverse[:, :k], in_order(own, image, other), ((1,), (0,)))
    basis[...] = v
    out[...] = own_rows(own, v)


def residual_kernel(items, core, inverse, cross, raw, other, basis, out):
    k = basis.shape[0]
    own = core[0] == 0
    inv = inverse[:, :k]
    projected = dot(dot(inv, cross[:, :k] / items, ((1,), (0,))), inv, ((1,), (1,)))
    product = dot(own_rows(own, inv), in_order(own, raw, other), ((1,), (0,)))
    out[...] = product - dot(own_rows(own, projected.T), basis[...], ((1,), (0,)))


def swap(x, axis, bit):
    n = lax.axis_size(axis)
    return lax.ppermute(x, axis, [(i, i ^ bit) for i in range(n)])


def swap_cross(x, first, second):
    n = lax.axis_size("col")
    pairs = []
    for c in range(n):
        pairs.append((c * 2, (c ^ first) * 2))
        pairs.append((c * 2 + 1, (c ^ second) * 2 + 1))
    return lax.ppermute(x, ("col", "cuts"), pairs)


def gather(x):
    far = swap(x, "row", 2)
    near = swap(x, "row", 1)
    last = swap(far, "row", 1)
    return {rel: (v, swap(v, "cuts", 1)) for rel, v in ((0, x), (1, near), (2, far), (3, last))}


def reduce_cuts(acc, ncol):
    n = acc.shape[0] // 2
    got = swap(acc[n:], "cuts", 1)
    step = n // ncol
    return [
        lax.optimization_barrier(acc[q * step:(q + 1) * step] + got[q * step:(q + 1) * step])
        for q in range(ncol)
    ]


def over_col(sent):
    far = swap_cross(sent[2], 3, 3)
    one = swap_cross(sent[0], 2, 1)
    two = swap_cross(sent[1], 1, 2)
    return one, two, far


def reduce_col(parts, rider=None):
    if rider is None:
        one, two, far = over_col(parts[1:])
        return parts[0] + one + two + far
    n = parts[0].shape[0]
    one, two, far = over_col([jnp.concatenate([v, rider[None]]) for v in parts[1:]])
    rest = rider + one[n] + two[n] + far[n]
    return parts[0] + one[:n] + two[:n] + far[:n], rest


def total(x, order):
    for axis, bit in order:
        x = x + swap(x, axis, bit)
    return x


def schedule(tile_rows, tile_cols, seg_blocks):
    ncol = lax.axis_size("col")
    r, c, a = (lax.axis_index(n) for n in ("row", "col", "cuts"))
    half = seg_blocks // 2
    slots = tile_rows.shape[0]
    rel = (tile_cols // seg_blocks // ncol) ^ r
    colp = rel * seg_blocks + tile_cols % seg_blocks
    local = tile_rows - r * ncol * seg_blocks
    live = tile_rows >= 0
    d = (local // seg_blocks) ^ c
    owner = local % seg_blocks // half
    place = jnp.where(owner == 0, d // 2 + d % 2 * 2, d)
    rowp = ((owner ^ a) * ncol + place) * half + local % half
    key = jnp.where(live, (rel + 1) // 2, len(PASSES))
    ids = lax.iota(jnp.int32, slots)
    rank = key * slots + ids
    place_of = jnp.sum((rank[None, :] < rank[:, None]).astype(jnp.int32), axis=1)
    onehot = place_of[None, :] == ids[:, None]
    packed = jnp.where(live, rowp * 256 + colp, 0)
    order = jnp.sum(jnp.where(onehot, ids[None, :], 0), axis=1)
    packed = jnp.sum(jnp.where(onehot, packed[None, :], 0), axis=1)
    marks = lax.iota(jnp.int32, len(PASSES) + 1)
    edges = jnp.sum((key[None, :] < marks[:, None]).astype(jnp.int32), axis=1)
    return order, packed // 256, packed % 256, edges


def fast_shards(warm, tiles, tile_rows, tile_cols):
    ncol, nrow = lax.axis_size("col"), lax.axis_size("row")
    block = tiles.shape[1]
    kloc, width = warm.shape
    k = 2 * kloc
    seg_blocks = width // block
    out_blocks = ncol * seg_blocks
    items = width * nrow * ncol
    core = jnp.reshape(lax.axis_index("cuts"), (1,)).astype(jnp.int32)

    x = call(enter_kernel, f32((seg_blocks * kloc, block)), 0, warm)
    staged = stage(tiles)
    index = schedule(tile_rows, tile_cols, seg_blocks)
    sizes = (k, out_blocks, seg_blocks)
    acc = operator(core, index, staged, gather(x), *sizes, False)
    image = reduce_col(reduce_cuts(acc, ncol))

    panel = gather(image)
    beside = swap_cross(image, 2, 1)
    across = swap_cross(jnp.concatenate([image, beside]), 1, 2)
    acc = operator(core, index, staged, panel, *sizes, True)
    parts = reduce_cuts(acc, ncol)
    gram = 0.0
    for rels in PASSES:
        gram += outer([x for rel in rels for x in panel[rel]], [])
    cross = outer([image, beside, across], parts)
    cross = total(cross, (("row", 1), ("row", 2), ("cuts", 1)))
    cross = reduce_col([cross] * ncol)
    raw, gram = reduce_col(parts, gram)
    inverse = call(functools.partial(inverse_kernel, items), f32((k, 128)), 0, gram)
    basis_all, basis = call(
        basis_kernel, (f32((k, width)), f32((kloc, width))), 1,
        core, inverse, *panel[0],
    )
    other = swap(raw, "cuts", 1)
    residual = call(
        functools.partial(residual_kernel, items), f32((kloc, width)), 1,
        core, inverse, cross, raw, other, basis_all,
    )
    return basis, residual


def block_product(panel, tiles, rows, positions, base, out_blocks):
    count_rows = panel.shape[0]
    block = tiles.shape[1]
    blocks = panel.reshape(count_rows, -1, block)
    picked = jnp.take(blocks, positions, axis=1)
    prods = jnp.einsum("suv,ksv->ksu", tiles, picked, precision=HIGHEST)
    local = rows - base
    onehot = (local[:, None] == jnp.arange(out_blocks, dtype=jnp.int32)[None, :]).astype(
        jnp.float32
    )
    summed = jnp.einsum("ksu,sb->kbu", prods, onehot, precision=HIGHEST)
    return summed.reshape(count_rows, out_blocks * block)


def operator_apply(vectors, tiles, rows, positions, base, out_blocks):
    panel = lax.all_gather(vectors, "row", axis=1, tiled=True)
    panel = lax.all_gather(panel, "cuts", axis=0, tiled=True)
    partial_value = block_product(panel, tiles, rows, positions, base, out_blocks)
    partial_value = lax.psum_scatter(partial_value, "cuts", scatter_dimension=0, tiled=True)
    return lax.psum_scatter(partial_value, "col", scatter_dimension=1, tiled=True)


def any_shards(warm, tiles, tile_rows, tile_cols):
    ncol = lax.axis_size("col")
    nrow = lax.axis_size("row")
    block = tiles.shape[1]
    seg_blocks = warm.shape[1] // block
    out_blocks = ncol * seg_blocks
    items = warm.shape[1] * nrow * ncol
    base = lax.axis_index("row") * out_blocks
    segment = tile_cols // seg_blocks
    positions = segment // ncol * seg_blocks + tile_cols % seg_blocks
    image = operator_apply(warm, tiles, tile_rows, positions, base, out_blocks)
    whole = lax.all_gather(image, "cuts", axis=0, tiled=True)
    gram = lax.psum(dot(whole, whole, ((1,), (1,))), ("row", "col")) / items
    lower = jnp.linalg.cholesky(gram)
    kloc = warm.shape[0]
    start = lax.axis_index("cuts") * kloc
    inverse = lax.linalg.triangular_solve(
        lower, jnp.eye(whole.shape[0], dtype=jnp.float32), left_side=True, lower=True
    )
    mine_rows = lax.dynamic_slice_in_dim(inverse, start, kloc, 0)
    basis = dot(mine_rows, whole, ((1,), (0,)))
    basis_all = lax.all_gather(basis, "cuts", axis=0, tiled=True)
    product = operator_apply(basis, tiles, tile_rows, positions, base, out_blocks)
    projected = lax.psum(dot(basis_all, product, ((1,), (1,))), ("row", "col")) / items
    residual = product - dot(projected, basis_all, ((0,), (0,)))
    return (basis, residual)


def solution(mesh):
    sizes = tuple(mesh.shape[n] for n in ("row", "col", "cuts"))
    fast = sizes == (4, 4, 2)
    return jax.shard_map(
        fast_shards if fast else any_shards,
        mesh=mesh,
        in_specs=(
            P("cuts", ("row", "col")),
            P(("row", "col", "cuts"), None, None),
            P(("row", "col", "cuts")),
            P(("row", "col", "cuts")),
        ),
        out_specs=(P("cuts", ("row", "col")), P("cuts", ("row", "col"))),
        check_vma=False,
    )
```
